32 devices in a mesh: op: 4 (over z), row: 8 (over y, x, core).
Axes of the slice: x: 2, y: 2, z: 4, core: 2. Of those that a mesh axis runs over, the one named last changes fastest.
Arguments:
- wannier_ops: bfloat16 [2, 1000, 2, 128, 128], P(None, 'row'), may hold values from -0.1875 to 0.1875
- r_coords: int32 [1000, 3], P('row'), may hold values from -8 to 8
- degeneracy: int32 [1000], P('row'), may hold values from 1 to 4
- kpoints: int32 [64, 3], replicated, may hold values from 0 to 15
- bloch_vectors: bfloat16 [64, 2, 64, 128], P(('op', 'row')), may hold values from -0.375 to 0.375
Outputs:
- covariant: float32 [64, 2, 4096], P(('op', 'row'))
The draws below stay inside these ranges and needn't reach their ends.
Inputs may be any that keep to these rules, and one draw needn't show every extreme that they name: `r_coords`: these coordinates are small integers; a program may pack several of them into one int32 word when it moves them. `degeneracy`: these degeneracies are small integers; a program may pack several of them into one int32 word when it moves them.
All inputs are finite; a program needn't handle non-finite values.
Results may differ from the reference program's by a relative error of at most 0.0038.
Values may be sent and summed in bfloat16 or wider, within the bound.
A program may use at most 192 MiB of HBM per device.

```python
import math
import jax
import jax.numpy as jnp
from jax import lax

W = 128
NB = 64
GRID = 16
RMAX = 8
NR = 1000
K = 64


def place_ends(entries, rng, least, top_value):
    longest = entries.shape.index(max(entries.shape))
    spots = []
    for shift in (0, 1):
        where = [jax.random.randint(jax.random.fold_in(rng, axis), (), 0, length) for axis, length in enumerate(entries.shape)]
        where[longest] = (where[longest] + shift) % entries.shape[longest]
        spots.append(tuple(where))
    return entries.at[spots[0]].set(least).at[spots[1]].set(top_value)


def block_levels(key, dims, split, smallest, high):
    factor_of, own = 1.0, jax.random.fold_in(key, 6)
    for position, parts in split:
        heights = jnp.exp(jax.random.uniform(jax.random.fold_in(own, position), (parts,), jnp.float32, smallest / len(split), high / len(split)))
        factor_of = factor_of * jnp.repeat(heights, dims[position] // parts).reshape([-1 if axis == position else 1 for axis in range(len(dims))])
    return factor_of


def scatter_about(rng, shape, scale, most, split=(), kind=jnp.bfloat16):
    drawn = jax.random.normal(rng, shape, jnp.float32) * scale
    if len(split) > 0:
        drawn = block_levels(rng, shape, split, -0.22, 0.18) * drawn
    return jnp.clip(drawn, min=-most, max=most).astype(kind)


def setup_inputs(seed: int = 0) -> dict:
    key_of = jax.random.split(jax.random.key(seed), 6)
    wannier_ops = scatter_about(key_of[0], (2, NR, 2, W, W), NR ** -0.5, 0.1875, ((1, 8),))
    r_coords = place_ends(jax.random.randint(key_of[1], (NR, 3), -RMAX, RMAX + 1), jax.random.fold_in(key_of[1], 1), -RMAX, RMAX).astype(jnp.int32)
    degeneracy = place_ends(jax.random.randint(key_of[2], (NR,), 1, 5), jax.random.fold_in(key_of[2], 1), 1, 4).astype(jnp.int32)
    kpoints = place_ends(jax.random.randint(key_of[3], (K, 3), 0, GRID), jax.random.fold_in(key_of[3], 1), 0, GRID - 1).astype(jnp.int32)
    bloch_vectors = scatter_about(key_of[4], (K, 2, NB, W), (2 * W) ** -0.5, 0.375, ((0, 32),))
    return dict(wannier_ops=wannier_ops, r_coords=r_coords, degeneracy=degeneracy, kpoints=kpoints, bloch_vectors=bloch_vectors)


TWO_PI = 6.283185307179586
HIGH = lax.Precision.HIGHEST

def phase_parts(r_coords, degeneracy, kpoints):
    turns_int = lax.optimization_barrier(jnp.sum(r_coords[:, None, :] * kpoints[None, :, :], axis=2)) % GRID
    angles = turns_int.astype(jnp.float32) * (TWO_PI / GRID)
    weights = 1.0 / degeneracy.astype(jnp.float32)
    cosine = jnp.cos(angles) * weights[:, None]
    sine_part = jnp.sin(angles) * weights[:, None]
    along_x = (r_coords[:, 0].astype(jnp.float32) / RMAX)[:, None]
    return (cosine, sine_part, along_x)

def fourier(phase_re, phase_im, flat_ops):
    stacked = jnp.concatenate([phase_re, phase_im], axis=1)
    product_sum = lax.dot_general(stacked, flat_ops, (((0,), (0,)), ((), ())), preferred_element_type=jnp.float32)
    k_count = phase_re.shape[1]
    half_cols = flat_ops.shape[1] // 2
    real_part = product_sum[:k_count, :half_cols] - product_sum[k_count:, half_cols:]
    imag_part = product_sum[:k_count, half_cols:] + product_sum[k_count:, :half_cols]
    return (real_part, imag_part)

def complex_mul(form, left, right):

    def single(first, second):
        return jnp.einsum(form, first, second, precision=HIGH)
    return (single(left[0], right[0]) - single(left[1], right[1]), single(left[0], right[1]) + single(left[1], right[0]))

def rotate(op_pair, vec_pair):
    left_side = complex_mul('knm,kmp->knp', (vec_pair[0], -vec_pair[1]), op_pair)
    return complex_mul('knm,kpm->knp', left_side, vec_pair)

def covariant_form(ham, deriv, posit, posit_deriv):
    band_count = ham[0].shape[-1]
    factor = 1.0 / math.sqrt(band_count)
    form = 'kab,kbc->kac'
    a_d = complex_mul(form, posit, deriv)
    d_a = complex_mul(form, deriv, posit)
    h_a = complex_mul(form, ham, posit)
    a_h = complex_mul(form, posit, ham)
    g_real = posit_deriv[0] + factor * (h_a[0] + a_h[0] - (a_d[1] - d_a[1]))
    g_imag = posit_deriv[1] + factor * (h_a[1] + a_h[1] + (a_d[0] - d_a[0]))
    k_count = g_real.shape[0]
    return jnp.stack([g_real.reshape(k_count, -1), g_imag.reshape(k_count, -1)], axis=1)

def reference(wannier_ops, r_coords, degeneracy, kpoints, bloch_vectors):
    cosine, sine_part, along_x = phase_parts(r_coords, degeneracy, kpoints)
    vectors = bloch_vectors.astype(jnp.float32)
    vec_pair = (vectors[:, 0], vectors[:, 1])
    rotated = []
    for component_id in range(4):
        flat_ops = wannier_ops[component_id // 2].reshape(NR, 2 * W * W)
        if component_id % 2 == 1:
            phase_re = -along_x * sine_part
            phase_im = along_x * cosine
        else:
            phase_re = cosine
            phase_im = sine_part
        real_part, imag_part = fourier(phase_re.astype(jnp.bfloat16), phase_im.astype(jnp.bfloat16), flat_ops)
        rotated.append(rotate((real_part.reshape(K, W, W), imag_part.reshape(K, W, W)), vec_pair))
    return covariant_form(rotated[0], rotated[1], rotated[2], rotated[3])
```

```python
import functools
import math

import jax
import jax.numpy as jnp
from jax import lax
from jax.experimental import pallas as pl
from jax.experimental.pallas import tpu as pltpu
from jax.sharding import PartitionSpec as P

GRID = 16
RMAX = 8
TWO_PI = 6.283185307179586
STEP = 16
AHEAD = 6
PITCH_PAD = 8
MESH = pl.DeviceIdType.MESH
F32 = jnp.float32
BF16 = jnp.bfloat16
NT = (((1,), (1,)), ((), ()))
NN = (((1,), (0,)), ((), ()))


def mm(a, b, dims=NN, precision=None):
    return lax.dot_general(a, b, dims, preferred_element_type=F32, precision=precision)


def kernel(
    n, ops_ref, rc_ref, deg_ref, kp_ref, v_ref, out_ref,
    obuf, cast, phase, rcs, degs, fsum, vall, sbuf, rbuf, own,
    osem, lsem, vsend, vrecv, bsend, brecv,
):
    me = lax.axis_index("row")
    group = lax.axis_index("op")
    r_local, width = ops_ref.shape[1], ops_ref.shape[-1]
    r_pad = cast.shape[0]
    pitch = cast.shape[1]
    bands = v_ref.shape[2]
    per = v_ref.shape[0]
    k_group = n * per
    rows = 4 * k_group
    fpitch = fsum.shape[1]
    blocks = width // STEP
    total = 2 * blocks

    def op_copy(t):
        return pltpu.make_async_copy(
            ops_ref.at[t // blocks, :, :, pl.ds((t % blocks) * STEP, STEP), :],
            obuf.at[t],
            osem.at[t],
        )

    for t in range(min(AHEAD, total)):
        op_copy(t).start()

    barrier = pltpu.get_barrier_semaphore()

    def greet(s, carry):
        pl.semaphore_signal(barrier, inc=1, device_id={"row": lax.rem(me + s, n)}, device_id_type=MESH)
        return carry

    lax.fori_loop(1, n, greet, 0)

    local_v = pltpu.make_async_copy(v_ref, vall.at[me], lsem)
    local_v.start()

    rcs[...] = jnp.zeros_like(rcs)
    rcs[pl.ds(0, r_local), :] = rc_ref[...].astype(F32)
    degs[...] = jnp.ones_like(degs)
    degs[:, pl.ds(0, r_local)] = deg_ref[...].astype(F32)
    coords = rcs[...].astype(BF16)
    points = kp_ref[pl.ds(pl.multiple_of(group * k_group, k_group), k_group), :].astype(F32).astype(BF16)
    inner = mm(points, coords, NT)
    pick = (lax.broadcasted_iota(jnp.int32, points.shape, 1) == 0).astype(F32).astype(BF16)
    along_x = mm(pick, coords, NT) / RMAX
    turns = inner - GRID * jnp.floor(inner / GRID)
    angles = turns * (TWO_PI / GRID)
    live = lax.broadcasted_iota(jnp.int32, inner.shape, 1) < r_local
    weights = jnp.where(live, 1.0 / degs[...], 0.0)
    cosine = jnp.cos(angles) * weights
    sine = jnp.sin(angles) * weights
    for comp, (re, im) in enumerate(((cosine, sine), (-along_x * sine, along_x * cosine))):
        base = comp * 2 * k_group
        phase[pl.ds(base, k_group), :] = jnp.concatenate([re, -im], axis=1).astype(BF16)
        phase[pl.ds(base + k_group, k_group), :] = jnp.concatenate([im, re], axis=1).astype(BF16)
    if r_pad > r_local:
        cast[pl.ds(r_local, r_pad - r_local)] = jnp.zeros((r_pad - r_local, pitch, width), F32)

    pl.semaphore_wait(barrier, n - 1)

    def v_copy(s):
        to = lax.rem(me + s, n)
        return pltpu.make_async_remote_copy(
            src_ref=v_ref, dst_ref=vall.at[me], send_sem=vsend.at[to], recv_sem=vrecv.at[me],
            device_id={"row": to}, device_id_type=MESH,
        )

    def v_start(s, carry):
        v_copy(s).start()
        return carry

    lax.fori_loop(1, n, v_start, 0)

    cast_rows = cast.reshape(r_pad * pitch, width)
    fsum_rows = fsum.reshape(width * fpitch, width)

    def fourier(op):
        def body(i, carry):
            t = op * blocks + i
            op_copy(t).wait()

            @pl.when(t + AHEAD < total)
            def _():
                op_copy(t + AHEAD).start()

            cast[pl.ds(0, r_local), pl.ds(0, 2 * STEP), :] = (
                obuf[t].astype(F32).reshape(r_local, 2 * STEP, width)
            )
            left = phase[...]
            for q in range(0, STEP, 2):
                sides = []
                for m in (q, q + 1):
                    parts = [
                        cast_rows[pl.ds(p * STEP + m, r_pad, stride=pitch), :].astype(BF16)
                        for p in range(2)
                    ]
                    sides.append(jnp.concatenate(parts, axis=0))
                got = mm(left, jnp.concatenate(sides, axis=1))
                fsum[i * STEP + q, pl.ds(0, rows), :] = got[:, :width]
                fsum[i * STEP + q + 1, pl.ds(0, rows), :] = got[:, width:]
            return carry

        lax.fori_loop(0, blocks, body, 0)

    def band_blocks(owner, kk):
        v_re, v_im = vall[owner, kk, 0], vall[owner, kk, 1]
        first = jnp.concatenate([v_re, -v_im], axis=1)
        second = jnp.concatenate([v_im, v_re], axis=1)
        third = jnp.concatenate([-v_re, v_im], axis=1)
        right = jnp.concatenate([first, second, second, third], axis=0)
        lefts = []
        for comp in range(2):
            row = comp * 2 * k_group + owner * per + kk
            re = fsum_rows[pl.ds(row, width, stride=fpitch), :].astype(BF16)
            im = fsum_rows[pl.ds(row + k_group, width, stride=fpitch), :].astype(BF16)
            lefts.append(jnp.concatenate([re, im], axis=1))
        g = mm(jnp.concatenate(lefts, axis=0), right, NT).astype(BF16)
        cols = 2 * bands
        stacks = [
            jnp.concatenate(
                [g[c * width:(c + 1) * width, :cols], g[c * width:(c + 1) * width, cols:]], axis=0
            )
            for c in range(2)
        ]
        b = mm(jnp.concatenate([v_re, v_im], axis=1), jnp.concatenate(stacks, axis=1))
        return b[:, :cols], b[:, cols:]

    def b_copy(op, to):
        return pltpu.make_async_remote_copy(
            src_ref=sbuf.at[op, to], dst_ref=rbuf.at[op, me],
            send_sem=bsend.at[op, to], recv_sem=brecv.at[op, me],
            device_id={"row": to}, device_id_type=MESH,
        )

    def v_wait(src):
        pltpu.make_async_remote_copy(
            src_ref=v_ref, dst_ref=vall.at[src], send_sem=vsend.at[src], recv_sem=vrecv.at[src],
            device_id={"row": src}, device_id_type=MESH,
        ).wait()

    def b_wait(op, src):
        pltpu.make_async_remote_copy(
            src_ref=sbuf.at[op, src], dst_ref=rbuf.at[op, src],
            send_sem=bsend.at[op, src], recv_sem=brecv.at[op, src],
            device_id={"row": src}, device_id_type=MESH,
        ).wait()

    for op in range(2):
        fourier(op)

        def send(s, carry):
            to = lax.rem(me + s, n)
            if op == 0:
                v_wait(to)
            for kk in range(per):
                for comp, b in enumerate(band_blocks(to, kk)):
                    sbuf[op, to, kk, comp] = b.astype(BF16)
            b_copy(op, to).start()
            return carry

        lax.fori_loop(1, n, send, 0)
        if op == 0:
            local_v.wait()
        for kk in range(per):
            for comp, b in enumerate(band_blocks(me, kk)):
                own[op, kk, comp] = b

    for op in range(2):

        def take(s, carry):
            src = lax.rem(me + s, n)
            b_wait(op, src)
            own[op] = own[op] + rbuf[op, src].astype(F32)
            return carry

        lax.fori_loop(1, n, take, 0)

    factor = 1.0 / math.sqrt(bands)

    def turn(m):
        return jnp.concatenate([-m[:, bands:], m[:, :bands]], axis=1)

    for kk in range(per):
        ham, deriv, posit, last = own[0, kk, 0], own[0, kk, 1], own[1, kk, 0], own[1, kk, 1]
        i_deriv = turn(deriv)
        plus, minus = ham + i_deriv, ham - i_deriv
        left = jnp.concatenate([posit, minus], axis=1)
        right = jnp.concatenate([plus, turn(plus), posit, turn(posit)], axis=0)
        res = last + factor * mm(left, right, NN, lax.Precision.HIGHEST)
        out_ref[kk, 0] = res[:, :bands]
        out_ref[kk, 1] = res[:, bands:]


def on_device(wannier_ops, r_coords, degeneracy, kpoints, bloch_vectors):
    n = lax.axis_size("row")
    r_local, width = wannier_ops.shape[1], wannier_ops.shape[-1]
    per, _, bands, _ = bloch_vectors.shape
    r_pad = -(-r_local // 128) * 128
    k_group = n * per
    total = 2 * (width // STEP)
    vmem = pl.BlockSpec(memory_space=pltpu.VMEM)
    dma = pltpu.SemaphoreType.DMA
    res = pl.pallas_call(
        functools.partial(kernel, n),
        out_shape=jax.ShapeDtypeStruct((per, 2, bands, bands), F32),
        in_specs=[pl.BlockSpec(memory_space=pl.ANY), vmem, vmem, vmem, vmem],
        out_specs=vmem,
        scratch_shapes=[
            pltpu.VMEM((total, r_local, 2, STEP, width), BF16),
            pltpu.VMEM((r_pad, 2 * STEP + PITCH_PAD, width), F32),
            pltpu.VMEM((4 * k_group, 2 * r_pad), BF16),
            pltpu.VMEM((r_pad, 3), F32),
            pltpu.VMEM((1, r_pad), F32),
            pltpu.VMEM((width, 4 * k_group + PITCH_PAD, width), F32),
            pltpu.VMEM((n, per, 2, bands, width), BF16),
            pltpu.VMEM((2, n, per, 2, bands, 2 * bands), BF16),
            pltpu.VMEM((2, n, per, 2, bands, 2 * bands), BF16),
            pltpu.VMEM((2, per, 2, bands, 2 * bands), F32),
            dma((total,)),
            dma,
            dma((n,)),
            dma((n,)),
            dma((2, n)),
            dma((2, n)),
        ],
        compiler_params=pltpu.CompilerParams(
            collective_id=0, has_side_effects=True, vmem_limit_bytes=62 * 1024 * 1024
        ),
    )(wannier_ops, r_coords, degeneracy.reshape(1, r_local), kpoints, bloch_vectors)
    return res.reshape(per, 2, bands * bands)


def solution(mesh):
    in_specs = (
        P(None, "row", None, None, None),
        P("row", None),
        P("row"),
        P(),
        P(("op", "row"), None, None, None),
    )
    out_specs = P(("op", "row"), None, None)
    return jax.shard_map(
        on_device, mesh=mesh, in_specs=in_specs, out_specs=out_specs, check_vma=False
    )
```

```python
import functools
import math

import jax
import jax.numpy as jnp
from jax import lax
from jax.experimental import pallas as pl
from jax.experimental.pallas import tpu as pltpu
from jax.sharding import PartitionSpec as P

GRID = 16
RMAX = 8
TWO_PI = 6.283185307179586
STEP = 16
AHEAD = 6
PITCH_PAD = 8
MESH = pl.DeviceIdType.MESH
F32 = jnp.float32
BF16 = jnp.bfloat16
NT = (((1,), (1,)), ((), ()))
NN = (((1,), (0,)), ((), ()))


def mm(a, b, dims=NN, precision=None):
    return lax.dot_general(a, b, dims, preferred_element_type=F32, precision=precision)


def kernel(
    n, ops_ref, rc_ref, deg_ref, kp_ref, v_ref, out_ref,
    obuf, cast, phase, rcs, kps, inners, degs, fsum, vall, sbuf, rbuf, own,
    osem, lsem, vsend, vrecv, bsend, brecv,
):
    me = lax.axis_index("row")
    group = lax.axis_index("op")
    r_local, width = ops_ref.shape[1], ops_ref.shape[-1]
    r_pad = cast.shape[0]
    pitch = cast.shape[1]
    bands = v_ref.shape[2]
    per = v_ref.shape[0]
    k_group = n * per
    rows = 4 * k_group
    fpitch = fsum.shape[1]
    blocks = width // STEP
    total = 2 * blocks

    def op_copy(t):
        return pltpu.make_async_copy(
            ops_ref.at[t // blocks, :, :, pl.ds((t % blocks) * STEP, STEP), :],
            obuf.at[t],
            osem.at[t],
        )

    for t in range(min(AHEAD, total)):
        op_copy(t).start()

    barrier = pltpu.get_barrier_semaphore()

    def greet(s, carry):
        pl.semaphore_signal(barrier, inc=1, device_id={"row": lax.rem(me + s, n)}, device_id_type=MESH)
        return carry

    lax.fori_loop(1, n, greet, 0)

    local_v = pltpu.make_async_copy(v_ref, vall.at[me], lsem)
    local_v.start()

    rcs[...] = jnp.zeros_like(rcs)
    rcs[pl.ds(0, 3), pl.ds(0, r_local)] = rc_ref[...].astype(F32)
    kps[...] = jnp.zeros_like(kps)
    kps[pl.ds(0, 3), :] = kp_ref[...].astype(F32)
    degs[...] = jnp.ones_like(degs)
    degs[:, pl.ds(0, r_local)] = deg_ref[...].astype(F32)
    coords = rcs[...].astype(BF16)
    inners[...] = mm(kps[...].astype(BF16), coords, (((0,), (0,)), ((), ())))
    inner = inners[pl.ds(pl.multiple_of(group * k_group, k_group), k_group), :]
    along_x = rcs[pl.ds(0, 1), :] / RMAX
    turns = inner - GRID * jnp.floor(inner / GRID)
    angles = turns * (TWO_PI / GRID)
    live = lax.broadcasted_iota(jnp.int32, inner.shape, 1) < r_local
    weights = jnp.where(live, 1.0 / degs[...], 0.0)
    cosine = jnp.cos(angles) * weights
    sine = jnp.sin(angles) * weights
    for comp, (re, im) in enumerate(((cosine, sine), (-along_x * sine, along_x * cosine))):
        base = comp * 2 * k_group
        phase[pl.ds(base, k_group), :] = jnp.concatenate([re, -im], axis=1).astype(BF16)
        phase[pl.ds(base + k_group, k_group), :] = jnp.concatenate([im, re], axis=1).astype(BF16)
    if r_pad > r_local:
        cast[pl.ds(r_local, r_pad - r_local)] = jnp.zeros((r_pad - r_local, pitch, width), F32)

    pl.semaphore_wait(barrier, n - 1)

    def v_copy(s):
        to = lax.rem(me + s, n)
        return pltpu.make_async_remote_copy(
            src_ref=v_ref, dst_ref=vall.at[me], send_sem=vsend.at[to], recv_sem=vrecv.at[me],
            device_id={"row": to}, device_id_type=MESH,
        )

    def v_start(s, carry):
        v_copy(s).start()
        return carry

    lax.fori_loop(1, n, v_start, 0)

    cast_rows = cast.reshape(r_pad * pitch, width)
    fsum_rows = fsum.reshape(width * fpitch, width)

    def fourier(op):
        def body(i, carry):
            t = op * blocks + i
            op_copy(t).wait()

            @pl.when(t + AHEAD < total)
            def _():
                op_copy(t + AHEAD).start()

            cast[pl.ds(0, r_local), pl.ds(0, 2 * STEP), :] = (
                obuf[t].astype(F32).reshape(r_local, 2 * STEP, width)
            )
            left = phase[...]
            for q in range(0, STEP, 2):
                sides = []
                for m in (q, q + 1):
                    parts = [
                        cast_rows[pl.ds(p * STEP + m, r_pad, stride=pitch), :].astype(BF16)
                        for p in range(2)
                    ]
                    sides.append(jnp.concatenate(parts, axis=0))
                got = mm(left, jnp.concatenate(sides, axis=1))
                fsum[i * STEP + q, pl.ds(0, rows), :] = got[:, :width]
                fsum[i * STEP + q + 1, pl.ds(0, rows), :] = got[:, width:]
            return carry

        lax.fori_loop(0, blocks, body, 0)

    def band_blocks(owner, kk):
        v_re, v_im = vall[owner, kk, 0], vall[owner, kk, 1]
        first = jnp.concatenate([v_re, -v_im], axis=1)
        second = jnp.concatenate([v_im, v_re], axis=1)
        third = jnp.concatenate([-v_re, v_im], axis=1)
        right = jnp.concatenate([first, second, second, third], axis=0)
        lefts = []
        for comp in range(2):
            row = comp * 2 * k_group + owner * per + kk
            re = fsum_rows[pl.ds(row, width, stride=fpitch), :].astype(BF16)
            im = fsum_rows[pl.ds(row + k_group, width, stride=fpitch), :].astype(BF16)
            lefts.append(jnp.concatenate([re, im], axis=1))
        g = mm(jnp.concatenate(lefts, axis=0), right, NT).astype(BF16)
        cols = 2 * bands
        stacks = [
            jnp.concatenate(
                [g[c * width:(c + 1) * width, :cols], g[c * width:(c + 1) * width, cols:]], axis=0
            )
            for c in range(2)
        ]
        b = mm(jnp.concatenate([v_re, v_im], axis=1), jnp.concatenate(stacks, axis=1))
        return b[:, :cols], b[:, cols:]

    def b_copy(op, to):
        return pltpu.make_async_remote_copy(
            src_ref=sbuf.at[op, to], dst_ref=rbuf.at[op, me],
            send_sem=bsend.at[op, to], recv_sem=brecv.at[op, me],
            device_id={"row": to}, device_id_type=MESH,
        )

    def v_wait(src):
        pltpu.make_async_remote_copy(
            src_ref=v_ref, dst_ref=vall.at[src], send_sem=vsend.at[src], recv_sem=vrecv.at[src],
            device_id={"row": src}, device_id_type=MESH,
        ).wait()

    def b_wait(op, src):
        pltpu.make_async_remote_copy(
            src_ref=sbuf.at[op, src], dst_ref=rbuf.at[op, src],
            send_sem=bsend.at[op, src], recv_sem=brecv.at[op, src],
            device_id={"row": src}, device_id_type=MESH,
        ).wait()

    for op in range(2):
        fourier(op)

        def send(s, carry):
            to = lax.rem(me + s, n)
            if op == 0:
                v_wait(to)
            for kk in range(per):
                for comp, b in enumerate(band_blocks(to, kk)):
                    sbuf[op, to, kk, comp] = b.astype(BF16)
            b_copy(op, to).start()
            return carry

        lax.fori_loop(1, n, send, 0)
        if op == 0:
            local_v.wait()
        for kk in range(per):
            for comp, b in enumerate(band_blocks(me, kk)):
                own[op, kk, comp] = b

    for op in range(2):

        def take(s, carry):
            src = lax.rem(me + s, n)
            b_wait(op, src)
            own[op] = own[op] + rbuf[op, src].astype(F32)
            return carry

        lax.fori_loop(1, n, take, 0)

    factor = 1.0 / math.sqrt(bands)

    def turn(m):
        return jnp.concatenate([-m[:, bands:], m[:, :bands]], axis=1)

    for kk in range(per):
        ham, deriv, posit, last = own[0, kk, 0], own[0, kk, 1], own[1, kk, 0], own[1, kk, 1]
        i_deriv = turn(deriv)
        plus, minus = ham + i_deriv, ham - i_deriv
        left = jnp.concatenate([posit, minus], axis=1)
        right = jnp.concatenate([plus, turn(plus), posit, turn(posit)], axis=0)
        res = last + factor * mm(left, right, NN, lax.Precision.HIGHEST)
        out_ref[kk, 0] = res[:, :bands]
        out_ref[kk, 1] = res[:, bands:]


def on_device(wannier_ops, r_coords, degeneracy, kpoints, bloch_vectors):
    n = lax.axis_size("row")
    r_local, width = wannier_ops.shape[1], wannier_ops.shape[-1]
    per, _, bands, _ = bloch_vectors.shape
    r_pad = -(-r_local // 128) * 128
    k_group = n * per
    total = 2 * (width // STEP)
    vmem = pl.BlockSpec(memory_space=pltpu.VMEM)
    dma = pltpu.SemaphoreType.DMA
    res = pl.pallas_call(
        functools.partial(kernel, n),
        out_shape=jax.ShapeDtypeStruct((per, 2, bands, bands), F32),
        in_specs=[pl.BlockSpec(memory_space=pl.ANY), vmem, vmem, vmem, vmem],
        out_specs=vmem,
        scratch_shapes=[
            pltpu.VMEM((total, r_local, 2, STEP, width), BF16),
            pltpu.VMEM((r_pad, 2 * STEP + PITCH_PAD, width), F32),
            pltpu.VMEM((4 * k_group, 2 * r_pad), BF16),
            pltpu.VMEM((8, r_pad), F32),
            pltpu.VMEM((8, kpoints.shape[0]), F32),
            pltpu.VMEM((kpoints.shape[0], r_pad), F32),
            pltpu.VMEM((1, r_pad), F32),
            pltpu.VMEM((width, 4 * k_group + PITCH_PAD, width), F32),
            pltpu.VMEM((n, per, 2, bands, width), BF16),
            pltpu.VMEM((2, n, per, 2, bands, 2 * bands), BF16),
            pltpu.VMEM((2, n, per, 2, bands, 2 * bands), BF16),
            pltpu.VMEM((2, per, 2, bands, 2 * bands), F32),
            dma((total,)),
            dma,
            dma((n,)),
            dma((n,)),
            dma((2, n)),
            dma((2, n)),
        ],
        compiler_params=pltpu.CompilerParams(
            collective_id=0, has_side_effects=True, vmem_limit_bytes=62 * 1024 * 1024
        ),
    )(wannier_ops, r_coords.T, degeneracy.reshape(1, r_local), kpoints.T, bloch_vectors)
    return res.reshape(per, 2, bands * bands)


def solution(mesh):
    in_specs = (
        P(None, "row", None, None, None),
        P("row", None),
        P("row"),
        P(),
        P(("op", "row"), None, None, None),
    )
    out_specs = P(("op", "row"), None, None)
    return jax.shard_map(
        on_device, mesh=mesh, in_specs=in_specs, out_specs=out_specs, check_vma=False
    )
```

```python
import functools
import math

import jax
import jax.numpy as jnp
from jax import lax
from jax.experimental import pallas as pl
from jax.experimental.pallas import tpu as pltpu
from jax.sharding import PartitionSpec as P

GRID = 16
RMAX = 8
TWO_PI = 6.283185307179586
STEP = 16
AHEAD = 6
PITCH_PAD = 8
MESH = pl.DeviceIdType.MESH
F32 = jnp.float32
BF16 = jnp.bfloat16
NT = (((1,), (1,)), ((), ()))
NN = (((1,), (0,)), ((), ()))


def mm(a, b, dims=NN, precision=None):
    return lax.dot_general(a, b, dims, preferred_element_type=F32, precision=precision)


def kernel(
    n, ops_ref, rc_ref, deg_ref, kp_ref, v_ref, out_ref,
    obuf, cast, phase, rcs, kps, inners, degs, fsum, vall, sbuf, rbuf, own,
    osem, lsem, vsend, vrecv, bsend, brecv,
):
    me = lax.axis_index("row")
    group = lax.axis_index("op")
    r_local, width = ops_ref.shape[1], ops_ref.shape[-1]
    pitch = 2 * STEP + 1
    r_pad = cast.shape[0] // pitch
    bands = v_ref.shape[2]
    per = v_ref.shape[0]
    k_group = n * per
    rows = 4 * k_group
    fpitch = fsum.shape[1]
    blocks = width // STEP
    total = 2 * blocks

    def op_copy(t):
        return pltpu.make_async_copy(
            ops_ref.at[t // blocks, :, :, pl.ds((t % blocks) * STEP, STEP), :],
            obuf.at[t],
            osem.at[t],
        )

    for t in range(min(AHEAD, total)):
        op_copy(t).start()

    barrier = pltpu.get_barrier_semaphore()

    def greet(s, carry):
        pl.semaphore_signal(barrier, inc=1, device_id={"row": lax.rem(me + s, n)}, device_id_type=MESH)
        return carry

    lax.fori_loop(1, n, greet, 0)

    local_v = pltpu.make_async_copy(v_ref, vall.at[me], lsem)
    local_v.start()

    rcs[...] = jnp.zeros_like(rcs)
    rcs[pl.ds(0, 3), pl.ds(0, r_local)] = rc_ref[...].astype(F32)
    kps[...] = jnp.zeros_like(kps)
    kps[pl.ds(0, 3), :] = kp_ref[...].astype(F32)
    degs[...] = jnp.ones_like(degs)
    degs[:, pl.ds(0, r_local)] = deg_ref[...].astype(F32)
    coords = rcs[...].astype(BF16)
    inners[...] = mm(kps[...].astype(BF16), coords, (((0,), (0,)), ((), ())))
    inner = inners[pl.ds(pl.multiple_of(group * k_group, k_group), k_group), :]
    along_x = rcs[pl.ds(0, 1), :] / RMAX
    turns = inner - GRID * jnp.floor(inner / GRID)
    angles = turns * (TWO_PI / GRID)
    live = lax.broadcasted_iota(jnp.int32, inner.shape, 1) < r_local
    weights = jnp.where(live, 1.0 / degs[...], 0.0)
    cosine = jnp.cos(angles) * weights
    sine = jnp.sin(angles) * weights
    for comp, (re, im) in enumerate(((cosine, sine), (-along_x * sine, along_x * cosine))):
        base = comp * 2 * k_group
        phase[pl.ds(base, k_group), :] = jnp.concatenate([re, -im], axis=1).astype(BF16)
        phase[pl.ds(base + k_group, k_group), :] = jnp.concatenate([im, re], axis=1).astype(BF16)
    if r_pad > r_local:
        tail = (r_pad - r_local) * pitch
        cast[pl.ds(r_local * pitch, tail), :] = jnp.zeros((tail, width), F32)

    pl.semaphore_wait(barrier, n - 1)

    def v_copy(s):
        to = lax.rem(me + s, n)
        return pltpu.make_async_remote_copy(
            src_ref=v_ref, dst_ref=vall.at[me], send_sem=vsend.at[to], recv_sem=vrecv.at[me],
            device_id={"row": to}, device_id_type=MESH,
        )

    def v_start(s, carry):
        v_copy(s).start()
        return carry

    lax.fori_loop(1, n, v_start, 0)

    cast_rows = cast
    fsum_rows = fsum.reshape(width * fpitch, width)

    def fourier(op):
        def body(i, carry):
            t = op * blocks + i
            op_copy(t).wait()

            @pl.when(t + AHEAD < total)
            def _():
                op_copy(t + AHEAD).start()

            for r in range(r_local):
                cast[pl.ds(r * pitch, 2 * STEP), :] = (
                    obuf[t, r].astype(F32).reshape(2 * STEP, width)
                )
            left = phase[...]
            for q in range(0, STEP, 2):
                sides = []
                for m in (q, q + 1):
                    parts = [
                        cast_rows[pl.ds(p * STEP + m, r_pad, stride=pitch), :].astype(BF16)
                        for p in range(2)
                    ]
                    sides.append(jnp.concatenate(parts, axis=0))
                got = mm(left, jnp.concatenate(sides, axis=1))
                fsum[i * STEP + q, pl.ds(0, rows), :] = got[:, :width]
                fsum[i * STEP + q + 1, pl.ds(0, rows), :] = got[:, width:]
            return carry

        lax.fori_loop(0, blocks, body, 0)

    def band_blocks(owner, kk):
        v_re, v_im = vall[owner, kk, 0], vall[owner, kk, 1]
        first = jnp.concatenate([v_re, -v_im], axis=1)
        second = jnp.concatenate([v_im, v_re], axis=1)
        third = jnp.concatenate([-v_re, v_im], axis=1)
        right = jnp.concatenate([first, second, second, third], axis=0)
        lefts = []
        for comp in range(2):
            row = comp * 2 * k_group + owner * per + kk
            re = fsum_rows[pl.ds(row, width, stride=fpitch), :].astype(BF16)
            im = fsum_rows[pl.ds(row + k_group, width, stride=fpitch), :].astype(BF16)
            lefts.append(jnp.concatenate([re, im], axis=1))
        g = mm(jnp.concatenate(lefts, axis=0), right, NT).astype(BF16)
        cols = 2 * bands
        stacks = [
            jnp.concatenate(
                [g[c * width:(c + 1) * width, :cols], g[c * width:(c + 1) * width, cols:]], axis=0
            )
            for c in range(2)
        ]
        b = mm(jnp.concatenate([v_re, v_im], axis=1), jnp.concatenate(stacks, axis=1))
        return b[:, :cols], b[:, cols:]

    def b_copy(op, to):
        return pltpu.make_async_remote_copy(
            src_ref=sbuf.at[op, to], dst_ref=rbuf.at[op, me],
            send_sem=bsend.at[op, to], recv_sem=brecv.at[op, me],
            device_id={"row": to}, device_id_type=MESH,
        )

    def v_wait(src):
        pltpu.make_async_remote_copy(
            src_ref=v_ref, dst_ref=vall.at[src], send_sem=vsend.at[src], recv_sem=vrecv.at[src],
            device_id={"row": src}, device_id_type=MESH,
        ).wait()

    def b_wait(op, src):
        pltpu.make_async_remote_copy(
            src_ref=sbuf.at[op, src], dst_ref=rbuf.at[op, src],
            send_sem=bsend.at[op, src], recv_sem=brecv.at[op, src],
            device_id={"row": src}, device_id_type=MESH,
        ).wait()

    for op in range(2):
        fourier(op)

        def send(s, carry):
            to = lax.rem(me + s, n)
            if op == 0:
                v_wait(to)
            for kk in range(per):
                for comp, b in enumerate(band_blocks(to, kk)):
                    sbuf[op, to, kk, comp] = b.astype(BF16)
            b_copy(op, to).start()
            return carry

        lax.fori_loop(1, n, send, 0)
        if op == 0:
            local_v.wait()
        for kk in range(per):
            for comp, b in enumerate(band_blocks(me, kk)):
                own[op, kk, comp] = b

    for op in range(2):

        def take(s, carry):
            src = lax.rem(me + s, n)
            b_wait(op, src)
            own[op] = own[op] + rbuf[op, src].astype(F32)
            return carry

        lax.fori_loop(1, n, take, 0)

    factor = 1.0 / math.sqrt(bands)

    def turn(m):
        return jnp.concatenate([-m[:, bands:], m[:, :bands]], axis=1)

    for kk in range(per):
        ham, deriv, posit, last = own[0, kk, 0], own[0, kk, 1], own[1, kk, 0], own[1, kk, 1]
        i_deriv = turn(deriv)
        plus, minus = ham + i_deriv, ham - i_deriv
        left = jnp.concatenate([posit, minus], axis=1)
        right = jnp.concatenate([plus, turn(plus), posit, turn(posit)], axis=0)
        res = last + factor * mm(left, right, NN, lax.Precision.HIGHEST)
        out_ref[kk, 0] = res[:, :bands]
        out_ref[kk, 1] = res[:, bands:]


def on_device(wannier_ops, r_coords, degeneracy, kpoints, bloch_vectors):
    n = lax.axis_size("row")
    r_local, width = wannier_ops.shape[1], wannier_ops.shape[-1]
    per, _, bands, _ = bloch_vectors.shape
    r_pad = -(-r_local // 128) * 128
    k_group = n * per
    total = 2 * (width // STEP)
    vmem = pl.BlockSpec(memory_space=pltpu.VMEM)
    dma = pltpu.SemaphoreType.DMA
    res = pl.pallas_call(
        functools.partial(kernel, n),
        out_shape=jax.ShapeDtypeStruct((per, 2, bands, bands), F32),
        in_specs=[pl.BlockSpec(memory_space=pl.ANY), vmem, vmem, vmem, vmem],
        out_specs=vmem,
        scratch_shapes=[
            pltpu.VMEM((total, r_local, 2, STEP, width), BF16),
            pltpu.VMEM((r_pad * (2 * STEP + 1), width), F32),
            pltpu.VMEM((4 * k_group, 2 * r_pad), BF16),
            pltpu.VMEM((8, r_pad), F32),
            pltpu.VMEM((8, kpoints.shape[0]), F32),
            pltpu.VMEM((kpoints.shape[0], r_pad), F32),
            pltpu.VMEM((1, r_pad), F32),
            pltpu.VMEM((width, 4 * k_group + PITCH_PAD, width), F32),
            pltpu.VMEM((n, per, 2, bands, width), BF16),
            pltpu.VMEM((2, n, per, 2, bands, 2 * bands), BF16),
            pltpu.VMEM((2, n, per, 2, bands, 2 * bands), BF16),
            pltpu.VMEM((2, per, 2, bands, 2 * bands), F32),
            dma((total,)),
            dma,
            dma((n,)),
            dma((n,)),
            dma((2, n)),
            dma((2, n)),
        ],
        compiler_params=pltpu.CompilerParams(
            collective_id=0, has_side_effects=True, vmem_limit_bytes=62 * 1024 * 1024
        ),
    )(wannier_ops, r_coords.T, degeneracy.reshape(1, r_local), kpoints.T, bloch_vectors)
    return res.reshape(per, 2, bands * bands)


def solution(mesh):
    in_specs = (
        P(None, "row", None, None, None),
        P("row", None),
        P("row"),
        P(),
        P(("op", "row"), None, None, None),
    )
    out_specs = P(("op", "row"), None, None)
    return jax.shard_map(
        on_device, mesh=mesh, in_specs=in_specs, out_specs=out_specs, check_vma=False
    )
```
